32 devices in a mesh: sec: 2 (over x), el: 16 (over z, y, core).
Axes of the slice: x: 2, y: 2, z: 4, core: 2. Of those that a mesh axis runs over, the one named last changes fastest.
Arguments:
- green_lesser: bfloat16 [2, 256, 64, 2, 128], P('sec', 'el'), may hold values from -6 to 6
- green_greater: bfloat16 [2, 256, 64, 2, 128], P('sec', 'el'), may hold values from -6 to 6
- coulomb: bfloat16 [2, 2, 256, 256], P('sec'), may hold values from -0.375 to 0.375
- pattern: int32 [2, 64], replicated, may hold values from 0 to 511, as said below
Outputs:
- polar: bfloat16 [2, 256, 64, 2, 128], P('sec', 'el')
- screened: bfloat16 [2, 256, 2, 256, 256], P('sec', 'el')
The draws below stay inside these ranges and needn't reach their ends.
Inputs may be any that keep to these rules, and one draw needn't show every extreme that they name: `pattern`: each row lists 64 distinct tile positions in increasing order.
All inputs are finite; a program needn't handle non-finite values.
Results may differ from the reference program's by a relative error of at most 0.014.
Values may be sent and summed in bfloat16 or wider, within the bound.
A program may use at most 128 MiB of HBM per device.

```python
import jax
import jax.numpy as jnp
from jax import lax

NB = 256
E = 256
TR = 8
TC = 16
TILE = 128
TILES = 512
NT = 64
RANGE = 32
CAP = 32
N_SEC = 2


def pattern_row(row_key):
    noise_key, owner_key = jax.random.split(row_key)
    positions = jnp.arange(TILES, dtype=jnp.int32)
    tile_row = positions // (NB // TC)
    tile_column = positions % (NB // TC)
    offset = jnp.abs(tile_row * TR - tile_column * TC)
    banded = jnp.where(offset < NB // 4, 1 << 19, 0).astype(jnp.int32)
    noise = jax.random.randint(noise_key, (TILES,), 0, 1 << 19, dtype=jnp.int32)
    chosen = jax.random.randint(owner_key, (), 0, TILES // RANGE, dtype=jnp.int32)
    forced = jnp.logical_and(positions // RANGE == chosen, positions % RANGE < CAP)
    score = (noise + banded + jnp.where(forced, 1 << 21, 0).astype(jnp.int32)) * TILES + positions
    best = lax.top_k(score, NT)[1]
    return jnp.sort(best).astype(jnp.int32)


def draw_pattern(key, part):
    keys = jax.random.split(jax.random.fold_in(key, 7), N_SEC)
    return jax.vmap(pattern_row)(keys)


def levels(rng, extent, cuts, low, top_value):
    def one(position, blocks):
        steps = jax.random.uniform(jax.random.fold_in(jax.random.fold_in(rng, 6), position), (blocks,), jnp.float32, low / len(cuts), top_value / len(cuts))
        return jnp.repeat(jnp.exp(steps), extent[position] // blocks).reshape((-1,) + (1,) * (len(extent) - position - 1))

    level = one(*cuts[0])
    for cut in cuts[1:]:
        level = level * one(*cut)
    return level


def bell_draw(rng, extent, spread, bound, cuts=(), kind=jnp.bfloat16):
    result = spread * jax.random.normal(rng, extent, jnp.float32)
    if cuts:
        result = result * levels(rng, extent, cuts, -0.22, 0.18)
    return jnp.clip(result, -bound, bound).astype(kind)


def setup_inputs(seed: int = 0) -> dict:
    streams_of = jax.random.split(jax.random.key(seed), 5)
    return {
        "green_lesser": bell_draw(streams_of[0], (N_SEC, E, NT, 2, TILE), 1.0, 6.0, ((0, 2), (1, 16))),
        "green_greater": bell_draw(streams_of[1], (N_SEC, E, NT, 2, TILE), 1.0, 6.0, ((0, 2), (1, 16))),
        "coulomb": bell_draw(streams_of[2], (N_SEC, 2, NB, NB), NB ** -0.5, 0.375, ((0, 2),)),
        "pattern": draw_pattern(jax.random.fold_in(streams_of[4], 71), 0),
    }


def correlate_section(lesser, greater):
    first = lesser[:, :, 0, :].astype(jnp.float32) + 1j * lesser[:, :, 1, :].astype(jnp.float32)
    second = greater[:, :, 0, :].astype(jnp.float32) + 1j * greater[:, :, 1, :].astype(jnp.float32)
    spectrum_first = jnp.fft.fft(first, n=2 * E, axis=0)
    spectrum_second = jnp.fft.fft(second, n=2 * E, axis=0)
    series = jnp.fft.ifft(spectrum_first * jnp.conj(spectrum_second), axis=0)[:E]
    factor = E ** -0.5
    return jnp.stack([-jnp.imag(series) * factor, jnp.real(series) * factor], axis=2).astype(jnp.bfloat16)


def to_block(tiles):
    count = tiles.shape[0]
    shaped = tiles.reshape(count, NB // TR, NB // TC, 2, TR, TC)
    return shaped.transpose(0, 3, 1, 4, 2, 5).reshape(count, 2, NB, NB)


def place(polar_section, listed):
    tiles = jnp.zeros((E, TILES, 2, TILE), jnp.bfloat16).at[:, listed].set(polar_section)
    return to_block(tiles)


def sandwich(matrix, blocks):
    wide = matrix.astype(jnp.float32)
    left = jnp.einsum('ij,ecjk->ecik', wide, blocks.astype(jnp.float32)).astype(jnp.bfloat16)
    return jnp.einsum('ecik,lk->ecil', left.astype(jnp.float32), wide)


def reference(green_lesser, green_greater, coulomb, pattern):
    polar = lax.map(lambda pair: correlate_section(pair[0], pair[1]), (green_lesser, green_greater))
    blocks = lax.map(lambda pair: place(pair[0], pair[1]), (polar, pattern))
    empty = jnp.zeros_like(blocks[:1])
    padded = jnp.concatenate([empty, blocks, empty], axis=0)
    upper = coulomb[:, 1]
    lower = jnp.concatenate([jnp.zeros_like(upper[:1]), upper[:-1]], axis=0)

    def screen(section):
        before = lax.dynamic_index_in_dim(padded, section, 0, keepdims=False)
        middle = lax.dynamic_index_in_dim(padded, section + 1, 0, keepdims=False)
        after = lax.dynamic_index_in_dim(padded, section + 2, 0, keepdims=False)
        diagonal = lax.dynamic_index_in_dim(coulomb[:, 0], section, 0, keepdims=False)
        forward = lax.dynamic_index_in_dim(upper, section, 0, keepdims=False)
        backward = lax.dynamic_index_in_dim(lower, section, 0, keepdims=False)
        total = sandwich(diagonal, middle) + sandwich(forward, after) + sandwich(backward.T, before)
        return total.astype(jnp.bfloat16)

    screened = lax.map(screen, jnp.arange(N_SEC, dtype=jnp.int32))
    return polar, screened
```

```python
import functools

import jax
import jax.numpy as jnp
import numpy as np
from jax import lax
from jax.experimental import pallas as pl
from jax.experimental.pallas import tpu as pltpu
from jax.sharding import PartitionSpec as P

TR = 8
TC = 16
VMEM_LIMIT = 56 * 1024 * 1024


def halves(table):
    upper = table.astype(jnp.bfloat16)
    lower = (table - upper.astype(np.float32)).astype(jnp.bfloat16)
    return upper, lower


def tables(energies):
    length = 2 * energies
    phase = np.outer(np.arange(length), np.arange(energies)) % length
    phase = phase * (2.0 * np.pi / length)
    cosine = np.cos(phase).astype(np.float32)
    sine = np.sin(phase).astype(np.float32)
    forward = np.concatenate(halves(np.concatenate([cosine, sine], axis=1)), axis=1)
    inverse = np.concatenate(halves(np.concatenate([cosine.T, sine.T], axis=1)), axis=1)
    return jnp.asarray(forward), jnp.asarray(inverse)


def dot32(a, b):
    return jnp.dot(a, b, preferred_element_type=jnp.float32)


def correlate_kernel(factor, x_ref, forward_ref, inverse_ref, out_ref):
    width = x_ref.shape[1] // 4
    x = x_ref[...]
    lesser_r, lesser_i, greater_r, greater_i = (
        x[:, i * width : (i + 1) * width] for i in range(4)
    )
    top = jnp.concatenate([lesser_r, greater_r, lesser_i, greater_i], axis=1)
    bottom = jnp.concatenate([lesser_i, greater_i, -lesser_r, -greater_r], axis=1)
    stacked = jnp.concatenate([top, bottom, top, bottom], axis=0)
    z = dot32(forward_ref[...], stacked)
    lr, gr, li, gi = (z[:, i * width : (i + 1) * width] for i in range(4))
    pr = lr * gr + li * gi
    pi = li * gr - lr * gi
    product = jnp.concatenate(
        [jnp.concatenate([-pi, pr], axis=1), jnp.concatenate([-pr, -pi], axis=1)], axis=0
    )
    high = product.astype(jnp.bfloat16)
    low = (product - high.astype(jnp.float32)).astype(jnp.bfloat16)
    depth = product.shape[0]
    series = dot32(inverse_ref[...], jnp.concatenate([high, high], axis=0))
    series = series + dot32(inverse_ref[:, :depth], low)
    out_ref[...] = (series * factor).astype(jnp.bfloat16)


def correlate(x, slots):
    energies, columns = x.shape
    width = columns // slots
    forward, inverse = tables(energies)
    factor = 1.0 / (2 * energies * energies**0.5)
    return pl.pallas_call(
        functools.partial(correlate_kernel, factor),
        grid=(slots,),
        in_specs=[
            pl.BlockSpec((energies, width), lambda s: (0, s)),
            pl.BlockSpec(forward.shape, lambda s: (0, 0)),
            pl.BlockSpec(inverse.shape, lambda s: (0, 0)),
        ],
        out_specs=pl.BlockSpec((energies, width // 2), lambda s: (0, s)),
        out_shape=jax.ShapeDtypeStruct((energies, columns // 2), jnp.bfloat16),
        compiler_params=pltpu.CompilerParams(vmem_limit_bytes=VMEM_LIMIT),
    )(x, forward, inverse)


def screen_kernel(count, terms, batch, *refs):
    tile_refs = refs[:terms]
    matrix_ref, row_ref, col_ref, spread_ref, out_ref, picked_ref, mask_ref = refs[terms:]
    nb = matrix_ref.shape[1]

    @pl.when(pl.program_id(0) == 0)
    def _():
        for t in range(terms):
            depth = row_ref.shape[2]
            position = lax.broadcasted_iota(jnp.int32, (nb, depth), 0)
            chosen = jnp.where(position == row_ref[t], 1.0, 0.0).astype(jnp.bfloat16)
            picked_ref[t] = dot32(matrix_ref[t], chosen).astype(jnp.bfloat16)
            lane = lax.broadcasted_iota(jnp.int32, (count, nb), 1) // TC
            mask_ref[t] = jnp.where(lane == col_ref[t], 1.0, 0.0)

    left = [[[] for _ in range(2)] for _ in range(batch)]
    for t in range(terms):
        width = spread_ref.shape[0]
        rows = jnp.concatenate(
            [tile_refs[t][b, :, c * width : (c + 1) * width] for b in range(batch) for c in range(2)],
            axis=0,
        )
        wide = dot32(rows, spread_ref[...])
        mask = mask_ref[t]
        for b in range(batch):
            for c in range(2):
                start = (2 * b + c) * count
                pieces = [
                    (wide[start : start + count, r * nb : (r + 1) * nb] * mask).astype(jnp.bfloat16)
                    for r in range(TR)
                ]
                stacked = jnp.concatenate(pieces, axis=0)
                left[b][c].append(dot32(picked_ref[t], stacked).astype(jnp.bfloat16))
    right = jnp.concatenate([matrix_ref[t] for t in range(terms)], axis=1)
    for b in range(batch):
        for c in range(2):
            joined = jnp.concatenate(left[b][c], axis=1)
            total = lax.dot_general(
                joined, right, (((1,), (1,)), ((), ())), preferred_element_type=jnp.float32
            )
            out_ref[b, c] = total.astype(jnp.bfloat16)


def screen(tiles, matrices, listed):
    terms = len(tiles)
    energies, count, both = tiles[0].shape
    nb = matrices.shape[1]
    batch = 2 if energies % 2 == 0 else 1
    width = both // 2
    tile_row = listed // (nb // TC)
    tile_col = listed % (nb // TC)
    offsets = jnp.arange(TR, dtype=jnp.int32)
    row_index = (tile_row[:, None, :] * TR + offsets[None, :, None]).reshape(terms, 1, TR * count)
    col_index = tile_col[:, :, None]
    entry = np.arange(width)[:, None]
    column = np.arange(TR * nb)[None, :]
    spread = jnp.asarray(
        (entry == column // nb * TC + column % TC).astype(np.float32).astype(jnp.bfloat16)
    )
    whole = lambda shape: pl.BlockSpec(shape, lambda i: (0,) * len(shape))
    return pl.pallas_call(
        functools.partial(screen_kernel, count, terms, batch),
        grid=(energies // batch,),
        in_specs=[pl.BlockSpec((batch, count, both), lambda i: (i, 0, 0))] * terms
        + [whole(matrices.shape), whole(row_index.shape), whole(col_index.shape), whole(spread.shape)],
        out_specs=pl.BlockSpec((batch, 2, nb, nb), lambda i: (i, 0, 0, 0)),
        out_shape=jax.ShapeDtypeStruct((energies, 2, nb, nb), jnp.bfloat16),
        scratch_shapes=[
            pltpu.VMEM((terms, nb, TR * count), jnp.bfloat16),
            pltpu.VMEM((terms, count, nb), jnp.float32),
        ],
        compiler_params=pltpu.CompilerParams(vmem_limit_bytes=VMEM_LIMIT),
    )(*tiles, matrices, row_index, col_index, spread)


def on_device(sections, owners, green_lesser, green_greater, coulomb, pattern):
    _, local, count, _, width = green_lesser.shape
    slots = count // owners
    energies = local * owners
    section = lax.axis_index("sec")

    both = jnp.stack([green_lesser[0], green_greater[0]], axis=2)
    both = both.reshape(local, owners, slots * 4 * width).transpose(1, 0, 2)
    gathered = lax.all_to_all(both, "el", split_axis=0, concat_axis=0, tiled=True)
    owned = correlate(gathered.reshape(energies, slots * 4 * width), slots)
    back = lax.all_to_all(
        owned.reshape(owners, local, slots * 2 * width), "el", split_axis=0, concat_axis=0, tiled=True
    )
    polar = back.transpose(1, 0, 2).reshape(local, count, 2 * width)

    tiles = [polar]
    matrices = [coulomb[0, 0]]
    listed = [lax.dynamic_index_in_dim(pattern, section, 0, keepdims=False)]
    if sections == 2:
        swap = [(0, 1), (1, 0)]
        tiles.append(lax.ppermute(polar, "sec", swap))
        other = lax.ppermute(coulomb[0, 1], "sec", swap)
        matrices.append(jnp.where(section == 0, coulomb[0, 1], other.T))
        listed.append(lax.dynamic_index_in_dim(pattern, 1 - section, 0, keepdims=False))
    elif sections > 2:
        up = [(i, i + 1) for i in range(sections - 1)]
        down = [(i + 1, i) for i in range(sections - 1)]
        tiles.append(lax.ppermute(polar, "sec", up))
        tiles.append(lax.ppermute(polar, "sec", down))
        matrices.append(lax.ppermute(coulomb[0, 1], "sec", up).T)
        matrices.append(coulomb[0, 1])
        before = jnp.maximum(section - 1, 0)
        after = jnp.minimum(section + 1, sections - 1)
        listed.append(lax.dynamic_index_in_dim(pattern, before, 0, keepdims=False))
        listed.append(lax.dynamic_index_in_dim(pattern, after, 0, keepdims=False))
    screened = screen(tiles, jnp.stack(matrices), jnp.stack(listed))
    return polar.reshape(1, local, count, 2, width), screened[None]


def solution(mesh):
    in_specs = (
        P("sec", "el", None, None, None),
        P("sec", "el", None, None, None),
        P("sec", None, None, None),
        P(),
    )
    out_specs = (P("sec", "el", None, None, None), P("sec", "el", None, None, None))
    return jax.shard_map(
        functools.partial(on_device, mesh.shape["sec"], mesh.shape["el"]),
        mesh=mesh,
        in_specs=in_specs,
        out_specs=out_specs,
        check_vma=False,
    )
```

```python
import functools

import jax
import jax.numpy as jnp
import numpy as np
from jax import lax
from jax.experimental import pallas as pl
from jax.experimental.pallas import tpu as pltpu
from jax.sharding import PartitionSpec as P

TR = 8
TC = 16
VMEM_LIMIT = 56 * 1024 * 1024


def halves(table):
    upper = table.astype(jnp.bfloat16)
    lower = (table - upper.astype(np.float32)).astype(jnp.bfloat16)
    return upper, lower


def tables(energies):
    length = 2 * energies
    phase = np.outer(np.arange(length), np.arange(energies)) % length
    phase = phase * (2.0 * np.pi / length)
    cosine = np.cos(phase).astype(np.float32)
    sine = np.sin(phase).astype(np.float32)
    real = np.stack([cosine, sine], axis=2).reshape(length, length)
    imag = np.stack([-sine, cosine], axis=2).reshape(length, length)
    forward = np.concatenate(halves(np.concatenate([real, imag], axis=0)), axis=1)
    out_r = np.concatenate([-sine.T, -cosine.T], axis=1)
    out_i = np.concatenate([cosine.T, -sine.T], axis=1)
    inverse = np.stack([out_r, out_i], axis=1).reshape(length, 2 * length)
    return jnp.asarray(forward), jnp.asarray(np.concatenate(halves(inverse), axis=1))


def dot32(a, b):
    return jnp.dot(a, b, preferred_element_type=jnp.float32)


def correlate_slot(factor, lesser, greater, forward_ref, inverse_ref):
    energies, _, width = lesser.shape
    length = 2 * energies
    joined = jnp.concatenate(
        [lesser.reshape(length, width), greater.reshape(length, width)], axis=1
    )
    z = dot32(forward_ref[:, :length], joined) + dot32(forward_ref[:, length:], joined)
    lr, gr = z[:length, :width], z[:length, width:]
    li, gi = z[length:, :width], z[length:, width:]
    product = jnp.concatenate([lr * gr + li * gi, li * gr - lr * gi], axis=0)
    high = product.astype(jnp.bfloat16)
    low = (product - high.astype(jnp.float32)).astype(jnp.bfloat16)
    depth = 2 * length
    first = dot32(inverse_ref[:, :depth], jnp.concatenate([high, low], axis=1))
    series = first[:, :width] + first[:, width:] + dot32(inverse_ref[:, depth:], high)
    return (series * factor).astype(jnp.bfloat16).reshape(energies, 2, width)


def exchange_kernel(
    owners,
    sections,
    factor,
    lesser_ref,
    greater_ref,
    coupling_ref,
    forward_hbm,
    inverse_hbm,
    *refs,
):
    sides = 1 if sections == 2 else 2
    polar_ref = refs[0]
    beside_refs = refs[1 : 1 + sides]
    other_ref = refs[1 + sides]
    (
        x_ref,
        d_ref,
        forward_ref,
        inverse_ref,
        table_sem,
        in_send,
        in_recv,
        out_send,
        out_recv,
        side_send,
        side_recv,
        c_send,
        c_recv,
    ) = refs[2 + sides :]
    slots = x_ref.shape[0]
    local = polar_ref.shape[0]
    me = lax.axis_index("el")
    section = lax.axis_index("sec")
    mesh_id = pl.DeviceIdType.MESH
    if sections == 2:
        targets = [1 - section]
    else:
        targets = [
            lax.rem(section + 1, sections),
            lax.rem(section + sections - 1, sections),
        ]

    load_f = pltpu.make_async_copy(forward_hbm, forward_ref, table_sem.at[0])
    load_i = pltpu.make_async_copy(inverse_hbm, inverse_ref, table_sem.at[1])
    load_f.start()
    load_i.start()

    barrier = pltpu.get_barrier_semaphore()

    def greet(step, carry):
        peer = lax.rem(me + step, owners)
        pl.semaphore_signal(barrier, inc=1, device_id={"el": peer}, device_id_type=mesh_id)
        return carry

    lax.fori_loop(1, owners, greet, 0)
    for target in targets:
        pl.semaphore_signal(barrier, inc=1, device_id={"sec": target}, device_id_type=mesh_id)
    pl.semaphore_wait(barrier, owners - 1 + sides)

    mine = pl.ds(me * local, local)
    for slot in range(slots):
        for which, source in enumerate((lesser_ref, greater_ref)):

            def send(step, carry, slot=slot, which=which, source=source):
                peer = lax.rem(me + step, owners)
                pltpu.make_async_remote_copy(
                    src_ref=source.at[:, peer, slot],
                    dst_ref=x_ref.at[slot, which, mine],
                    send_sem=in_send.at[slot],
                    recv_sem=in_recv.at[slot],
                    device_id={"el": peer},
                    device_id_type=mesh_id,
                ).start()
                return carry

            pltpu.make_async_copy(
                source.at[:, me, slot], x_ref.at[slot, which, mine], in_recv.at[slot]
            ).start()
            lax.fori_loop(1, owners, send, 0)

    shared = pltpu.make_async_remote_copy(
        src_ref=coupling_ref,
        dst_ref=other_ref,
        send_sem=c_send,
        recv_sem=c_recv,
        device_id={"sec": targets[0]},
        device_id_type=mesh_id,
    )
    shared.start()
    load_f.wait()
    load_i.wait()

    def arrive(slot):
        whole = polar_ref.at[:, :, slot]
        pltpu.make_async_copy(whole, whole, out_recv.at[slot]).wait()

    def forward_copy(slot, side):
        return pltpu.make_async_remote_copy(
            src_ref=polar_ref.at[:, :, slot],
            dst_ref=beside_refs[side].at[:, :, slot],
            send_sem=side_send.at[side, slot],
            recv_sem=side_recv.at[side, slot],
            device_id={"sec": targets[side]},
            device_id_type=mesh_id,
        )

    def pass_on(slot):
        arrive(slot)
        for side in range(sides):
            forward_copy(slot, side).start()

    for slot in range(slots):
        whole = x_ref.at[slot]
        pltpu.make_async_copy(whole, whole, in_recv.at[slot]).wait()
        d_ref[slot] = correlate_slot(
            factor, x_ref[slot, 0], x_ref[slot, 1], forward_ref, inverse_ref
        )
        pltpu.make_async_copy(
            d_ref.at[slot, mine], polar_ref.at[:, me, slot], out_recv.at[slot]
        ).start()

        def give(step, carry, slot=slot):
            peer = lax.rem(me + step, owners)
            pltpu.make_async_remote_copy(
                src_ref=d_ref.at[slot, pl.ds(peer * local, local)],
                dst_ref=polar_ref.at[:, me, slot],
                send_sem=out_send.at[slot],
                recv_sem=out_recv.at[slot],
                device_id={"el": peer},
                device_id_type=mesh_id,
            ).start()
            return carry

        lax.fori_loop(1, owners, give, 0)
        if slot >= 2:
            pass_on(slot - 2)
    for slot in range(max(slots - 2, 0), slots):
        pass_on(slot)

    sent = (owners - 1) * local
    for slot in range(slots):
        part = x_ref.at[slot, :, pl.ds(0, sent)]
        pltpu.make_async_copy(part, part, in_send.at[slot]).wait()
        part = d_ref.at[slot, pl.ds(0, sent)]
        pltpu.make_async_copy(part, part, out_send.at[slot]).wait()
        for side in range(sides):
            forward_copy(slot, side).wait()
    shared.wait()


def exchange(owners, sections, lesser, greater, coupling):
    local, count, _, width = lesser.shape
    slots = count // owners
    energies = local * owners
    sides = 1 if sections == 2 else 2
    forward, inverse = tables(energies)
    split = (local, owners, slots, 2, width)
    tile_shape = jax.ShapeDtypeStruct(split, jnp.bfloat16)
    anywhere = pl.BlockSpec(memory_space=pl.ANY)
    near = pl.BlockSpec(memory_space=pltpu.VMEM)
    dma = pltpu.SemaphoreType.DMA
    return pl.pallas_call(
        functools.partial(
            exchange_kernel, owners, sections, 1.0 / (2 * energies * energies**0.5)
        ),
        in_specs=[anywhere] * 5,
        out_specs=[near] * (2 + sides),
        out_shape=[tile_shape] * (1 + sides)
        + [jax.ShapeDtypeStruct(coupling.shape, coupling.dtype)],
        scratch_shapes=[
            pltpu.VMEM((slots, 2, energies, 2, width), jnp.bfloat16),
            pltpu.VMEM((slots, energies, 2, width), jnp.bfloat16),
            pltpu.VMEM(forward.shape, jnp.bfloat16),
            pltpu.VMEM(inverse.shape, jnp.bfloat16),
            dma((2,)),
            dma((slots,)),
            dma((slots,)),
            dma((slots,)),
            dma((slots,)),
            dma((sides, slots)),
            dma((sides, slots)),
            dma(()),
            dma(()),
        ],
        compiler_params=pltpu.CompilerParams(
            collective_id=0, has_side_effects=True, vmem_limit_bytes=VMEM_LIMIT
        ),
    )(lesser.reshape(split), greater.reshape(split), coupling, forward, inverse)


def screen_kernel(count, terms, batch, *refs):
    tile_refs = refs[:terms]
    matrix_ref, row_ref, col_ref, spread_ref, out_ref, picked_ref, mask_ref = refs[terms:]
    nb = matrix_ref.shape[1]

    @pl.when(pl.program_id(0) == 0)
    def _():
        for t in range(terms):
            depth = row_ref.shape[2]
            position = lax.broadcasted_iota(jnp.int32, (nb, depth), 0)
            chosen = jnp.where(position == row_ref[t], 1.0, 0.0).astype(jnp.bfloat16)
            picked_ref[t] = dot32(matrix_ref[t], chosen).astype(jnp.bfloat16)
            lane = lax.broadcasted_iota(jnp.int32, (count, nb), 1) // TC
            mask_ref[t] = jnp.where(lane == col_ref[t], 1.0, 0.0)

    left = [[[] for _ in range(2)] for _ in range(batch)]
    for t in range(terms):
        width = spread_ref.shape[0]
        rows = jnp.concatenate(
            [tile_refs[t][b, :, c * width : (c + 1) * width] for b in range(batch) for c in range(2)],
            axis=0,
        )
        wide = dot32(rows, spread_ref[...])
        mask = mask_ref[t]
        for b in range(batch):
            for c in range(2):
                start = (2 * b + c) * count
                pieces = [
                    (wide[start : start + count, r * nb : (r + 1) * nb] * mask).astype(jnp.bfloat16)
                    for r in range(TR)
                ]
                stacked = jnp.concatenate(pieces, axis=0)
                left[b][c].append(dot32(picked_ref[t], stacked).astype(jnp.bfloat16))
    right = jnp.concatenate([matrix_ref[t] for t in range(terms)], axis=1)
    for b in range(batch):
        for c in range(2):
            joined = jnp.concatenate(left[b][c], axis=1)
            total = lax.dot_general(
                joined, right, (((1,), (1,)), ((), ())), preferred_element_type=jnp.float32
            )
            out_ref[b, c] = total.astype(jnp.bfloat16)


def screen(tiles, matrices, listed):
    terms = len(tiles)
    energies, count, both = tiles[0].shape
    nb = matrices.shape[1]
    batch = 2 if energies % 2 == 0 else 1
    width = both // 2
    tile_row = listed // (nb // TC)
    tile_col = listed % (nb // TC)
    offsets = jnp.arange(TR, dtype=jnp.int32)
    row_index = (tile_row[:, None, :] * TR + offsets[None, :, None]).reshape(terms, 1, TR * count)
    col_index = tile_col[:, :, None]
    entry = np.arange(width)[:, None]
    column = np.arange(TR * nb)[None, :]
    spread = jnp.asarray(
        (entry == column // nb * TC + column % TC).astype(np.float32).astype(jnp.bfloat16)
    )
    whole = lambda shape: pl.BlockSpec(shape, lambda i: (0,) * len(shape))
    return pl.pallas_call(
        functools.partial(screen_kernel, count, terms, batch),
        grid=(energies // batch,),
        in_specs=[pl.BlockSpec((batch, count, both), lambda i: (i, 0, 0))] * terms
        + [whole(matrices.shape), whole(row_index.shape), whole(col_index.shape), whole(spread.shape)],
        out_specs=pl.BlockSpec((batch, 2, nb, nb), lambda i: (i, 0, 0, 0)),
        out_shape=jax.ShapeDtypeStruct((energies, 2, nb, nb), jnp.bfloat16),
        scratch_shapes=[
            pltpu.VMEM((terms, nb, TR * count), jnp.bfloat16),
            pltpu.VMEM((terms, count, nb), jnp.float32),
        ],
        compiler_params=pltpu.CompilerParams(vmem_limit_bytes=VMEM_LIMIT),
    )(*tiles, matrices, row_index, col_index, spread)


def on_device(sections, owners, green_lesser, green_greater, coulomb, pattern):
    _, local, count, _, width = green_lesser.shape
    section = lax.axis_index("sec")
    polar, *beside, other = exchange(
        owners, sections, green_lesser[0], green_greater[0], coulomb[0, 1]
    )
    flat = lambda t: t.reshape(local, count, 2 * width)
    matrices = [coulomb[0, 0]]
    listed = [lax.dynamic_index_in_dim(pattern, section, 0, keepdims=False)]
    if sections == 2:
        matrices.append(jnp.where(section == 0, coulomb[0, 1], other.T))
        listed.append(lax.dynamic_index_in_dim(pattern, 1 - section, 0, keepdims=False))
    else:
        before = lax.rem(section + sections - 1, sections)
        after = lax.rem(section + 1, sections)
        matrices.append(jnp.where(section > 0, other.T, 0))
        matrices.append(jnp.where(section < sections - 1, coulomb[0, 1], 0))
        listed.append(lax.dynamic_index_in_dim(pattern, before, 0, keepdims=False))
        listed.append(lax.dynamic_index_in_dim(pattern, after, 0, keepdims=False))
    screened = screen(
        [flat(t) for t in (polar, *beside)], jnp.stack(matrices), jnp.stack(listed)
    )
    return polar.reshape(1, local, count, 2, width), screened[None]


def solution(mesh):
    in_specs = (
        P("sec", "el", None, None, None),
        P("sec", "el", None, None, None),
        P("sec", None, None, None),
        P(),
    )
    out_specs = (P("sec", "el", None, None, None), P("sec", "el", None, None, None))
    return jax.shard_map(
        functools.partial(on_device, mesh.shape["sec"], mesh.shape["el"]),
        mesh=mesh,
        in_specs=in_specs,
        out_specs=out_specs,
        check_vma=False,
    )
```

```python
import functools

import jax
import jax.numpy as jnp
import numpy as np
from jax import lax
from jax.experimental import pallas as pl
from jax.experimental.pallas import tpu as pltpu
from jax.sharding import PartitionSpec as P

TR = 8
TC = 16
VMEM_LIMIT = 56 * 1024 * 1024


def halves(table):
    upper = table.astype(jnp.bfloat16)
    lower = (table - upper.astype(np.float32)).astype(jnp.bfloat16)
    return upper, lower


def tables(energies):
    length = 2 * energies
    phase = np.outer(np.arange(length), np.arange(energies)) % length
    phase = phase * (2.0 * np.pi / length)
    cosine = np.cos(phase).astype(np.float32)
    sine = np.sin(phase).astype(np.float32)
    real = np.stack([cosine, sine], axis=2).reshape(length, length)
    imag = np.stack([-sine, cosine], axis=2).reshape(length, length)
    forward = np.concatenate(halves(np.concatenate([real, imag], axis=0)), axis=1)
    out_r = np.concatenate([-sine.T, -cosine.T], axis=1)
    out_i = np.concatenate([cosine.T, -sine.T], axis=1)
    inverse = np.stack([out_r, out_i], axis=1).reshape(length, 2 * length)
    return jnp.asarray(forward), jnp.asarray(np.concatenate(halves(inverse), axis=1))


def dot32(a, b):
    return jnp.dot(a, b, preferred_element_type=jnp.float32)


def correlate_slot(factor, lesser, greater, forward_ref, inverse_ref):
    energies, _, width = lesser.shape
    length = 2 * energies
    joined = jnp.concatenate(
        [lesser.reshape(length, width), greater.reshape(length, width)], axis=1
    )
    z = dot32(forward_ref[:, :length], joined) + dot32(forward_ref[:, length:], joined)
    lr, gr = z[:length, :width], z[:length, width:]
    li, gi = z[length:, :width], z[length:, width:]
    product = jnp.concatenate([lr * gr + li * gi, li * gr - lr * gi], axis=0)
    high = product.astype(jnp.bfloat16)
    low = (product - high.astype(jnp.float32)).astype(jnp.bfloat16)
    depth = 2 * length
    first = dot32(inverse_ref[:, :depth], jnp.concatenate([high, low], axis=1))
    series = first[:, :width] + first[:, width:] + dot32(inverse_ref[:, depth:], high)
    return (series * factor).astype(jnp.bfloat16).reshape(energies, 2, width)


def exchange_kernel(
    owners,
    sections,
    factor,
    lesser_ref,
    greater_ref,
    coulomb_ref,
    forward_hbm,
    inverse_hbm,
    *refs,
):
    sides = 1 if sections == 2 else 2
    polar_ref = refs[0]
    beside_refs = refs[1 : 1 + sides]
    other_ref = refs[1 + sides]
    (
        x_ref,
        d_ref,
        forward_ref,
        inverse_ref,
        table_sem,
        in_send,
        in_recv,
        out_send,
        out_recv,
        side_send,
        side_recv,
        c_send,
        c_recv,
    ) = refs[2 + sides :]
    slots = x_ref.shape[0]
    local = polar_ref.shape[0]
    me = lax.axis_index("el")
    section = lax.axis_index("sec")
    mesh_id = pl.DeviceIdType.MESH
    if sections == 2:
        targets = [1 - section]
    else:
        targets = [
            lax.rem(section + 1, sections),
            lax.rem(section + sections - 1, sections),
        ]

    load_f = pltpu.make_async_copy(forward_hbm, forward_ref, table_sem.at[0])
    load_i = pltpu.make_async_copy(inverse_hbm, inverse_ref, table_sem.at[1])
    load_f.start()
    load_i.start()

    barrier = pltpu.get_barrier_semaphore()

    def greet(step, carry):
        peer = lax.rem(me + step, owners)
        pl.semaphore_signal(barrier, inc=1, device_id={"el": peer}, device_id_type=mesh_id)
        return carry

    lax.fori_loop(1, owners, greet, 0)
    for target in targets:
        pl.semaphore_signal(barrier, inc=1, device_id={"sec": target}, device_id_type=mesh_id)
    pl.semaphore_wait(barrier, owners - 1 + sides)

    def peer_at(turn):
        away = (turn + 1) // 2 * (2 * (turn % 2) - 1)
        return lax.rem(me + owners // 2 + away, owners)

    mine = pl.ds(me * local, local)
    for slot in range(slots):
        for which, source in enumerate((lesser_ref, greater_ref)):

            def send(turn, carry, slot=slot, which=which, source=source):
                peer = peer_at(turn)
                pltpu.make_async_remote_copy(
                    src_ref=source.at[:, peer, slot],
                    dst_ref=x_ref.at[slot, which, mine],
                    send_sem=in_send.at[slot],
                    recv_sem=in_recv.at[slot],
                    device_id={"el": peer},
                    device_id_type=mesh_id,
                ).start()
                return carry

            pltpu.make_async_copy(
                source.at[:, me, slot], x_ref.at[slot, which, mine], in_recv.at[slot]
            ).start()
            lax.fori_loop(0, owners - 1, send, 0)

    shared = pltpu.make_async_remote_copy(
        src_ref=coulomb_ref.at[1],
        dst_ref=other_ref,
        send_sem=c_send,
        recv_sem=c_recv,
        device_id={"sec": targets[0]},
        device_id_type=mesh_id,
    )
    shared.start()
    load_f.wait()
    load_i.wait()

    def arrive(slot):
        whole = polar_ref.at[:, :, slot]
        pltpu.make_async_copy(whole, whole, out_recv.at[slot]).wait()

    def forward_copy(slot, side):
        return pltpu.make_async_remote_copy(
            src_ref=polar_ref.at[:, :, slot],
            dst_ref=beside_refs[side].at[:, :, slot],
            send_sem=side_send.at[side, slot],
            recv_sem=side_recv.at[side, slot],
            device_id={"sec": targets[side]},
            device_id_type=mesh_id,
        )

    def pass_on(slot):
        arrive(slot)
        for side in range(sides):
            forward_copy(slot, side).start()

    for slot in range(slots):
        whole = x_ref.at[slot]
        pltpu.make_async_copy(whole, whole, in_recv.at[slot]).wait()
        d_ref[slot] = correlate_slot(
            factor, x_ref[slot, 0], x_ref[slot, 1], forward_ref, inverse_ref
        )
        pltpu.make_async_copy(
            d_ref.at[slot, mine], polar_ref.at[:, me, slot], out_recv.at[slot]
        ).start()

        def give(turn, carry, slot=slot):
            peer = peer_at(turn)
            pltpu.make_async_remote_copy(
                src_ref=d_ref.at[slot, pl.ds(peer * local, local)],
                dst_ref=polar_ref.at[:, me, slot],
                send_sem=out_send.at[slot],
                recv_sem=out_recv.at[slot],
                device_id={"el": peer},
                device_id_type=mesh_id,
            ).start()
            return carry

        lax.fori_loop(0, owners - 1, give, 0)
        if slot >= 2:
            pass_on(slot - 2)
    for slot in range(max(slots - 2, 0), slots):
        pass_on(slot)

    sent = (owners - 1) * local
    for slot in range(slots):
        part = x_ref.at[slot, :, pl.ds(0, sent)]
        pltpu.make_async_copy(part, part, in_send.at[slot]).wait()
        part = d_ref.at[slot, pl.ds(0, sent)]
        pltpu.make_async_copy(part, part, out_send.at[slot]).wait()
        for side in range(sides):
            forward_copy(slot, side).wait()
    shared.wait()


def exchange(owners, sections, lesser, greater, coulomb):
    local, count, _, width = lesser.shape
    slots = count // owners
    energies = local * owners
    sides = 1 if sections == 2 else 2
    forward, inverse = tables(energies)
    split = (local, owners, slots, 2, width)
    tile_shape = jax.ShapeDtypeStruct(split, jnp.bfloat16)
    anywhere = pl.BlockSpec(memory_space=pl.ANY)
    near = pl.BlockSpec(memory_space=pltpu.VMEM)
    dma = pltpu.SemaphoreType.DMA
    return pl.pallas_call(
        functools.partial(
            exchange_kernel, owners, sections, 1.0 / (2 * energies * energies**0.5)
        ),
        in_specs=[anywhere] * 5,
        out_specs=[near] * (2 + sides),
        out_shape=[tile_shape] * (1 + sides)
        + [jax.ShapeDtypeStruct(coulomb.shape[1:], coulomb.dtype)],
        scratch_shapes=[
            pltpu.VMEM((slots, 2, energies, 2, width), jnp.bfloat16),
            pltpu.VMEM((slots, energies, 2, width), jnp.bfloat16),
            pltpu.VMEM(forward.shape, jnp.bfloat16),
            pltpu.VMEM(inverse.shape, jnp.bfloat16),
            dma((2,)),
            dma((slots,)),
            dma((slots,)),
            dma((slots,)),
            dma((slots,)),
            dma((sides, slots)),
            dma((sides, slots)),
            dma(()),
            dma(()),
        ],
        compiler_params=pltpu.CompilerParams(
            collective_id=0, has_side_effects=True, vmem_limit_bytes=VMEM_LIMIT
        ),
    )(lesser.reshape(split), greater.reshape(split), coulomb, forward, inverse)


def screen_setup(sections, coulomb_ref, other_ref, pattern_ref, right_ref, picked_ref, mask_ref):
    terms, count, nb = mask_ref.shape
    section = lax.axis_index("sec")
    lower = other_ref[...].astype(jnp.float32).T
    upper = coulomb_ref[1].astype(jnp.float32)
    matrices = [coulomb_ref[0].astype(jnp.float32)]
    if sections == 2:
        sources = [section, 1 - section]
        matrices.append(jnp.where(section == 0, upper, lower))
    else:
        sources = [
            section,
            lax.rem(section + sections - 1, sections),
            lax.rem(section + 1, sections),
        ]
        matrices.append(jnp.where(section > 0, lower, 0.0))
        matrices.append(jnp.where(section < sections - 1, upper, 0.0))
    position = lax.broadcasted_iota(jnp.int32, (nb, TR * count), 0)
    lane = lax.broadcasted_iota(jnp.int32, (count, nb), 1) // TC
    first = lax.broadcasted_iota(jnp.int32, (count, count), 0)
    second = lax.broadcasted_iota(jnp.int32, (count, count), 1)
    across = nb // TC
    for t in range(terms):
        listed = pattern_ref[pl.ds(sources[t], 1), :]
        row = jnp.concatenate([listed // across * TR + r for r in range(TR)], axis=1)
        chosen = jnp.where(position == row, 1.0, 0.0).astype(jnp.bfloat16)
        picked_ref[t] = dot32(matrices[t].astype(jnp.bfloat16), chosen).astype(jnp.bfloat16)
        column = jnp.sum(
            jnp.where(first == second, (listed % across).astype(jnp.float32), 0.0),
            axis=1,
            keepdims=True,
        ).astype(jnp.int32)
        mask_ref[t] = jnp.where(lane == column, 1.0, 0.0)
        right_ref[t * nb : (t + 1) * nb] = matrices[t].T.astype(jnp.bfloat16)


def screen_kernel(sections, terms, batch, *refs):
    tile_refs = refs[:terms]
    coulomb_ref, other_ref, pattern_ref, out_ref = refs[terms : terms + 4]
    right_ref, picked_ref, mask_ref, rows_ref = refs[terms + 4 :]
    _, count, nb = mask_ref.shape
    width = rows_ref.shape[-1]

    @pl.when(pl.program_id(0) == 0)
    def _():
        screen_setup(
            sections, coulomb_ref, other_ref, pattern_ref, right_ref, picked_ref, mask_ref
        )

    lane = lax.broadcasted_iota(jnp.int32, (count, width), 1) % TC
    joined = [[] for _ in range(batch * 2)]
    for t in range(terms):
        for b in range(batch):
            rows_ref[t, b] = tile_refs[t][b].reshape(2 * count, width).astype(jnp.float32)
        mask = mask_ref[t]
        for b in range(batch):
            for c in range(2):
                tile = rows_ref[t, b, pl.ds(c, count, stride=2), :]
                pieces = []
                for r in range(TR):
                    spread = jnp.take_along_axis(
                        tile, lane + r * TC, axis=1, mode="promise_in_bounds"
                    )
                    wide = jnp.concatenate([spread] * (nb // width), axis=1)
                    pieces.append((wide * mask).astype(jnp.bfloat16))
                stacked = jnp.concatenate(pieces, axis=0)
                joined[2 * b + c].append(dot32(picked_ref[t], stacked).astype(jnp.bfloat16))
    left = jnp.concatenate([jnp.concatenate(j, axis=1) for j in joined], axis=0)
    total = dot32(left, right_ref[...]).astype(jnp.bfloat16)
    out_ref[...] = total.reshape(batch, 2, nb, nb)


def screen(sections, tiles, coulomb, other, pattern):
    terms = len(tiles)
    energies, owners, slots, _, width = tiles[0].shape
    count = owners * slots
    nb = coulomb.shape[1]
    batch = 2 if energies % 2 == 0 else 1
    whole = lambda array: pl.BlockSpec(array.shape, lambda i: (0,) * array.ndim)
    return pl.pallas_call(
        functools.partial(screen_kernel, sections, terms, batch),
        grid=(energies // batch,),
        in_specs=[pl.BlockSpec((batch, owners, slots, 2, width), lambda i: (i, 0, 0, 0, 0))] * terms
        + [whole(coulomb), whole(other), whole(pattern)],
        out_specs=pl.BlockSpec((batch, 2, nb, nb), lambda i: (i, 0, 0, 0)),
        out_shape=jax.ShapeDtypeStruct((energies, 2, nb, nb), jnp.bfloat16),
        scratch_shapes=[
            pltpu.VMEM((terms * nb, nb), jnp.bfloat16),
            pltpu.VMEM((terms, nb, TR * count), jnp.bfloat16),
            pltpu.VMEM((terms, count, nb), jnp.float32),
            pltpu.VMEM((terms, batch, 2 * count, width), jnp.float32),
        ],
        compiler_params=pltpu.CompilerParams(vmem_limit_bytes=VMEM_LIMIT),
    )(*tiles, coulomb, other, pattern)


def on_device(sections, owners, green_lesser, green_greater, coulomb, pattern):
    _, local, count, _, width = green_lesser.shape
    polar, *beside, other = exchange(
        owners, sections, green_lesser[0], green_greater[0], coulomb[0]
    )
    screened = screen(sections, [polar, *beside], coulomb[0], other, pattern)
    return polar.reshape(1, local, count, 2, width), screened[None]


def solution(mesh):
    in_specs = (
        P("sec", "el", None, None, None),
        P("sec", "el", None, None, None),
        P("sec", None, None, None),
        P(),
    )
    out_specs = (P("sec", "el", None, None, None), P("sec", "el", None, None, None))
    return jax.shard_map(
        functools.partial(on_device, mesh.shape["sec"], mesh.shape["el"]),
        mesh=mesh,
        in_specs=in_specs,
        out_specs=out_specs,
        check_vma=False,
    )
```

```python
import functools

import jax
import jax.numpy as jnp
import numpy as np
from jax import lax
from jax.experimental import pallas as pl
from jax.experimental.pallas import tpu as pltpu
from jax.sharding import PartitionSpec as P

TR = 8
TC = 16
VMEM_LIMIT = 56 * 1024 * 1024


def halves(table):
    upper = table.astype(jnp.bfloat16)
    lower = (table - upper.astype(np.float32)).astype(jnp.bfloat16)
    return upper, lower


def tables(energies):
    length = 2 * energies
    phase = np.outer(np.arange(length), np.arange(energies)) % length
    phase = phase * (2.0 * np.pi / length)
    cosine = np.cos(phase).astype(np.float32)
    sine = np.sin(phase).astype(np.float32)
    real = np.stack([cosine, sine], axis=2).reshape(length, length)
    imag = np.stack([-sine, cosine], axis=2).reshape(length, length)
    forward = np.concatenate(halves(np.concatenate([real, imag], axis=0)), axis=1)
    out_r = np.concatenate([-sine.T, -cosine.T], axis=1)
    out_i = np.concatenate([cosine.T, -sine.T], axis=1)
    inverse = np.stack([out_r, out_i], axis=1).reshape(length, 2 * length)
    return jnp.asarray(forward), jnp.asarray(np.concatenate(halves(inverse), axis=1))


def dot32(a, b):
    return jnp.dot(a, b, preferred_element_type=jnp.float32)


def correlate_slot(factor, lesser, greater, forward_ref, inverse_ref):
    energies, _, width = lesser.shape
    length = 2 * energies
    joined = jnp.concatenate(
        [lesser.reshape(length, width), greater.reshape(length, width)], axis=1
    )
    z = dot32(forward_ref[:, :length], joined) + dot32(forward_ref[:, length:], joined)
    lr, gr = z[:length, :width], z[:length, width:]
    li, gi = z[length:, :width], z[length:, width:]
    product = jnp.concatenate([lr * gr + li * gi, li * gr - lr * gi], axis=0)
    high = product.astype(jnp.bfloat16)
    low = (product - high.astype(jnp.float32)).astype(jnp.bfloat16)
    depth = 2 * length
    first = dot32(inverse_ref[:, :depth], jnp.concatenate([high, low], axis=1))
    series = first[:, :width] + first[:, width:] + dot32(inverse_ref[:, depth:], high)
    return (series * factor).astype(jnp.bfloat16).reshape(energies, 2, width)


def exchange_kernel(
    owners,
    sections,
    factor,
    lesser_ref,
    greater_ref,
    coulomb_ref,
    forward_hbm,
    inverse_hbm,
    *refs,
):
    sides = 1 if sections == 2 else 2
    polar_ref = refs[0]
    beside_refs = refs[1 : 1 + sides]
    other_ref = refs[1 + sides]
    (
        x_ref,
        d_ref,
        forward_ref,
        inverse_ref,
        table_sem,
        in_send,
        in_recv,
        out_send,
        out_recv,
        side_send,
        side_recv,
        c_send,
        c_recv,
    ) = refs[2 + sides :]
    slots = x_ref.shape[0]
    local = polar_ref.shape[0]
    me = lax.axis_index("el")
    section = lax.axis_index("sec")
    mesh_id = pl.DeviceIdType.MESH
    if sections == 2:
        targets = [1 - section]
    else:
        targets = [
            lax.rem(section + 1, sections),
            lax.rem(section + sections - 1, sections),
        ]

    load_f = pltpu.make_async_copy(forward_hbm, forward_ref, table_sem.at[0])
    load_i = pltpu.make_async_copy(inverse_hbm, inverse_ref, table_sem.at[1])
    load_f.start()
    load_i.start()

    barrier = pltpu.get_barrier_semaphore()

    def greet(step, carry):
        peer = lax.rem(me + step, owners)
        pl.semaphore_signal(barrier, inc=1, device_id={"el": peer}, device_id_type=mesh_id)
        return carry

    lax.fori_loop(1, owners, greet, 0)
    for target in targets:
        pl.semaphore_signal(barrier, inc=1, device_id={"sec": target}, device_id_type=mesh_id)
    pl.semaphore_wait(barrier, owners - 1 + sides)

    def peer_at(turn):
        away = (turn + 1) // 2 * (2 * (turn % 2) - 1)
        return lax.rem(me + owners // 2 + away, owners)

    mine = pl.ds(me * local, local)
    for slot in range(slots):
        for which, source in enumerate((lesser_ref, greater_ref)):

            def send(turn, carry, slot=slot, which=which, source=source):
                peer = peer_at(turn)
                pltpu.make_async_remote_copy(
                    src_ref=source.at[:, peer, slot],
                    dst_ref=x_ref.at[slot, which, mine],
                    send_sem=in_send.at[slot],
                    recv_sem=in_recv.at[slot],
                    device_id={"el": peer},
                    device_id_type=mesh_id,
                ).start()
                return carry

            pltpu.make_async_copy(
                source.at[:, me, slot], x_ref.at[slot, which, mine], in_recv.at[slot]
            ).start()
            lax.fori_loop(0, owners - 1, send, 0)

    shared = pltpu.make_async_remote_copy(
        src_ref=coulomb_ref.at[1],
        dst_ref=other_ref,
        send_sem=c_send,
        recv_sem=c_recv,
        device_id={"sec": targets[0]},
        device_id_type=mesh_id,
    )
    shared.start()
    load_f.wait()
    load_i.wait()

    def arrive(slot):
        whole = polar_ref.at[:, :, slot]
        pltpu.make_async_copy(whole, whole, out_recv.at[slot]).wait()

    def forward_copy(slot, side):
        return pltpu.make_async_remote_copy(
            src_ref=polar_ref.at[:, :, slot],
            dst_ref=beside_refs[side].at[:, :, slot],
            send_sem=side_send.at[side, slot],
            recv_sem=side_recv.at[side, slot],
            device_id={"sec": targets[side]},
            device_id_type=mesh_id,
        )

    def pass_on(slot):
        arrive(slot)
        for side in range(sides):
            forward_copy(slot, side).start()

    for slot in range(slots):
        whole = x_ref.at[slot]
        pltpu.make_async_copy(whole, whole, in_recv.at[slot]).wait()
        d_ref[slot] = correlate_slot(
            factor, x_ref[slot, 0], x_ref[slot, 1], forward_ref, inverse_ref
        )
        pltpu.make_async_copy(
            d_ref.at[slot, mine], polar_ref.at[:, me, slot], out_recv.at[slot]
        ).start()

        def give(turn, carry, slot=slot):
            peer = peer_at(turn)
            pltpu.make_async_remote_copy(
                src_ref=d_ref.at[slot, pl.ds(peer * local, local)],
                dst_ref=polar_ref.at[:, me, slot],
                send_sem=out_send.at[slot],
                recv_sem=out_recv.at[slot],
                device_id={"el": peer},
                device_id_type=mesh_id,
            ).start()
            return carry

        lax.fori_loop(0, owners - 1, give, 0)
        if slot >= 2:
            pass_on(slot - 2)
    for slot in range(max(slots - 2, 0), slots):
        pass_on(slot)

    sent = (owners - 1) * local
    for slot in range(slots):
        part = x_ref.at[slot, :, pl.ds(0, sent)]
        pltpu.make_async_copy(part, part, in_send.at[slot]).wait()
        part = d_ref.at[slot, pl.ds(0, sent)]
        pltpu.make_async_copy(part, part, out_send.at[slot]).wait()
        for side in range(sides):
            forward_copy(slot, side).wait()
    shared.wait()


def exchange(owners, sections, lesser, greater, coulomb):
    local, count, _, width = lesser.shape
    slots = count // owners
    energies = local * owners
    sides = 1 if sections == 2 else 2
    forward, inverse = tables(energies)
    split = (local, owners, slots, 2, width)
    tile_shape = jax.ShapeDtypeStruct(split, jnp.bfloat16)
    anywhere = pl.BlockSpec(memory_space=pl.ANY)
    near = pl.BlockSpec(memory_space=pltpu.VMEM)
    dma = pltpu.SemaphoreType.DMA
    return pl.pallas_call(
        functools.partial(
            exchange_kernel, owners, sections, 1.0 / (2 * energies * energies**0.5)
        ),
        in_specs=[anywhere] * 5,
        out_specs=[near] * (2 + sides),
        out_shape=[tile_shape] * (1 + sides)
        + [jax.ShapeDtypeStruct(coulomb.shape[1:], coulomb.dtype)],
        scratch_shapes=[
            pltpu.VMEM((slots, 2, energies, 2, width), jnp.bfloat16),
            pltpu.VMEM((slots, energies, 2, width), jnp.bfloat16),
            pltpu.VMEM(forward.shape, jnp.bfloat16),
            pltpu.VMEM(inverse.shape, jnp.bfloat16),
            dma((2,)),
            dma((slots,)),
            dma((slots,)),
            dma((slots,)),
            dma((slots,)),
            dma((sides, slots)),
            dma((sides, slots)),
            dma(()),
            dma(()),
        ],
        compiler_params=pltpu.CompilerParams(
            collective_id=0, has_side_effects=True, vmem_limit_bytes=VMEM_LIMIT
        ),
    )(lesser.reshape(split), greater.reshape(split), coulomb, forward, inverse)


def screen_setup(sections, coulomb_ref, other_ref, pattern_ref, right_ref, picked_ref, mask_ref):
    terms, count, nb = mask_ref.shape
    section = lax.axis_index("sec")
    lower = other_ref[...].astype(jnp.float32).T
    upper = coulomb_ref[1].astype(jnp.float32)
    matrices = [coulomb_ref[0].astype(jnp.float32)]
    if sections == 2:
        sources = [section, 1 - section]
        matrices.append(jnp.where(section == 0, upper, lower))
    else:
        sources = [
            section,
            lax.rem(section + sections - 1, sections),
            lax.rem(section + 1, sections),
        ]
        matrices.append(jnp.where(section > 0, lower, 0.0))
        matrices.append(jnp.where(section < sections - 1, upper, 0.0))
    position = lax.broadcasted_iota(jnp.int32, (nb, TR * count), 0)
    lane = lax.broadcasted_iota(jnp.int32, (count, nb), 1) // TC
    first = lax.broadcasted_iota(jnp.int32, (count, count), 0)
    second = lax.broadcasted_iota(jnp.int32, (count, count), 1)
    across = nb // TC
    for t in range(terms):
        listed = pattern_ref[pl.ds(sources[t], 1), :]
        row = jnp.concatenate([listed // across * TR + r for r in range(TR)], axis=1)
        chosen = jnp.where(position == row, 1.0, 0.0).astype(jnp.bfloat16)
        picked_ref[t] = dot32(matrices[t].astype(jnp.bfloat16), chosen).astype(jnp.bfloat16)
        column = jnp.sum(
            jnp.where(first == second, (listed % across).astype(jnp.float32), 0.0),
            axis=1,
            keepdims=True,
        ).astype(jnp.int32)
        mask_ref[t] = jnp.where(lane == column, 1.0, 0.0).astype(jnp.bfloat16)
        right_ref[t * nb : (t + 1) * nb] = matrices[t].T.astype(jnp.bfloat16)


def screen_kernel(sections, terms, batch, *refs):
    tile_refs = refs[:terms]
    coulomb_ref, other_ref, pattern_ref, out_ref = refs[terms : terms + 4]
    right_ref, picked_ref, mask_ref, rows_ref = refs[terms + 4 :]
    _, count, nb = mask_ref.shape
    width = rows_ref.shape[-1]

    @pl.when(pl.program_id(0) == 0)
    def _():
        screen_setup(
            sections, coulomb_ref, other_ref, pattern_ref, right_ref, picked_ref, mask_ref
        )

    lane = lax.broadcasted_iota(jnp.int32, (count, width), 1) % TC
    joined = [[] for _ in range(batch * 2)]
    for t in range(terms):
        for b in range(batch):
            rows_ref[t, b] = tile_refs[t][b].reshape(2 * count, width).astype(jnp.float32)
        mask = mask_ref[t]
        for b in range(batch):
            for c in range(2):
                tile = rows_ref[t, b, pl.ds(c, count, stride=2), :]
                pieces = []
                for r in range(TR):
                    spread = jnp.take_along_axis(
                        tile, lane + r * TC, axis=1, mode="promise_in_bounds"
                    )
                    spread = spread.astype(jnp.bfloat16)
                    wide = jnp.concatenate([spread] * (nb // width), axis=1)
                    pieces.append(wide * mask)
                stacked = jnp.concatenate(pieces, axis=0)
                joined[2 * b + c].append(dot32(picked_ref[t], stacked).astype(jnp.bfloat16))
    left = jnp.concatenate([jnp.concatenate(j, axis=1) for j in joined], axis=0)
    total = dot32(left, right_ref[...]).astype(jnp.bfloat16)
    out_ref[...] = total.reshape(batch, 2, nb, nb)


def screen(sections, tiles, coulomb, other, pattern):
    terms = len(tiles)
    energies, owners, slots, _, width = tiles[0].shape
    count = owners * slots
    nb = coulomb.shape[1]
    batch = next(n for n in (4, 2, 1) if energies % n == 0)
    whole = lambda array: pl.BlockSpec(array.shape, lambda i: (0,) * array.ndim)
    return pl.pallas_call(
        functools.partial(screen_kernel, sections, terms, batch),
        grid=(energies // batch,),
        in_specs=[pl.BlockSpec((batch, owners, slots, 2, width), lambda i: (i, 0, 0, 0, 0))] * terms
        + [whole(coulomb), whole(other), whole(pattern)],
        out_specs=pl.BlockSpec((batch, 2, nb, nb), lambda i: (i, 0, 0, 0)),
        out_shape=jax.ShapeDtypeStruct((energies, 2, nb, nb), jnp.bfloat16),
        scratch_shapes=[
            pltpu.VMEM((terms * nb, nb), jnp.bfloat16),
            pltpu.VMEM((terms, nb, TR * count), jnp.bfloat16),
            pltpu.VMEM((terms, count, nb), jnp.bfloat16),
            pltpu.VMEM((terms, batch, 2 * count, width), jnp.float32),
        ],
        compiler_params=pltpu.CompilerParams(vmem_limit_bytes=VMEM_LIMIT),
    )(*tiles, coulomb, other, pattern)


def on_device(sections, owners, green_lesser, green_greater, coulomb, pattern):
    _, local, count, _, width = green_lesser.shape
    polar, *beside, other = exchange(
        owners, sections, green_lesser[0], green_greater[0], coulomb[0]
    )
    screened = screen(sections, [polar, *beside], coulomb[0], other, pattern)
    return polar.reshape(1, local, count, 2, width), screened[None]


def solution(mesh):
    in_specs = (
        P("sec", "el", None, None, None),
        P("sec", "el", None, None, None),
        P("sec", None, None, None),
        P(),
    )
    out_specs = (P("sec", "el", None, None, None), P("sec", "el", None, None, None))
    return jax.shard_map(
        functools.partial(on_device, mesh.shape["sec"], mesh.shape["el"]),
        mesh=mesh,
        in_specs=in_specs,
        out_specs=out_specs,
        check_vma=False,
    )
```

```python
import functools

import jax
import jax.numpy as jnp
import numpy as np
from jax import lax
from jax.experimental import pallas as pl
from jax.experimental.pallas import tpu as pltpu
from jax.sharding import PartitionSpec as P

TR = 8
TC = 16
VMEM_LIMIT = 56 * 1024 * 1024


def halves(table):
    upper = table.astype(jnp.bfloat16)
    lower = (table - upper.astype(np.float32)).astype(jnp.bfloat16)
    return upper, lower


def tables(energies):
    length = 2 * energies
    phase = np.outer(np.arange(length), np.arange(energies)) % length
    phase = phase * (2.0 * np.pi / length)
    cosine = np.cos(phase).astype(np.float32)
    sine = np.sin(phase).astype(np.float32)
    real = np.stack([cosine, sine], axis=2).reshape(length, length)
    imag = np.stack([-sine, cosine], axis=2).reshape(length, length)
    forward = np.concatenate(halves(np.concatenate([real, imag], axis=0)), axis=1)
    out_r = np.concatenate([-sine.T, -cosine.T], axis=1)
    out_i = np.concatenate([cosine.T, -sine.T], axis=1)
    inverse = np.stack([out_r, out_i], axis=1).reshape(length, 2 * length)
    return jnp.asarray(forward), jnp.asarray(np.concatenate(halves(inverse), axis=1))


def dot32(a, b):
    return jnp.dot(a, b, preferred_element_type=jnp.float32)


def correlate_slot(factor, lesser, greater, forward_ref, inverse_ref):
    energies, _, width = lesser.shape
    length = 2 * energies
    joined = jnp.concatenate(
        [lesser.reshape(length, width), greater.reshape(length, width)], axis=1
    )
    z = dot32(forward_ref[:, :length], joined) + dot32(forward_ref[:, length:], joined)
    lr, gr = z[:length, :width], z[:length, width:]
    li, gi = z[length:, :width], z[length:, width:]
    product = jnp.concatenate([lr * gr + li * gi, li * gr - lr * gi], axis=0)
    high = product.astype(jnp.bfloat16)
    low = (product - high.astype(jnp.float32)).astype(jnp.bfloat16)
    depth = 2 * length
    first = dot32(inverse_ref[:, :depth], jnp.concatenate([high, low], axis=1))
    series = first[:, :width] + first[:, width:] + dot32(inverse_ref[:, depth:], high)
    return (series * factor).astype(jnp.bfloat16).reshape(energies, 2, width)


def exchange_kernel(
    owners,
    sections,
    factor,
    lesser_ref,
    greater_ref,
    coulomb_ref,
    forward_hbm,
    inverse_hbm,
    *refs,
):
    sides = 1 if sections == 2 else 2
    polar_ref = refs[0]
    beside_refs = refs[1 : 1 + sides]
    other_ref = refs[1 + sides]
    (
        x_ref,
        d_ref,
        forward_ref,
        inverse_ref,
        table_sem,
        in_send,
        in_recv,
        out_send,
        out_recv,
        side_send,
        side_recv,
        c_send,
        c_recv,
    ) = refs[2 + sides :]
    slots = x_ref.shape[0]
    local = polar_ref.shape[0]
    me = lax.axis_index("el")
    section = lax.axis_index("sec")
    mesh_id = pl.DeviceIdType.MESH
    if sections == 2:
        targets = [1 - section]
    else:
        targets = [
            lax.rem(section + 1, sections),
            lax.rem(section + sections - 1, sections),
        ]

    load_f = pltpu.make_async_copy(forward_hbm, forward_ref, table_sem.at[0])
    load_i = pltpu.make_async_copy(inverse_hbm, inverse_ref, table_sem.at[1])
    load_f.start()
    load_i.start()

    barrier = pltpu.get_barrier_semaphore()

    def greet(step, carry):
        peer = lax.rem(me + step, owners)
        pl.semaphore_signal(barrier, inc=1, device_id={"el": peer}, device_id_type=mesh_id)
        return carry

    lax.fori_loop(1, owners, greet, 0)
    for target in targets:
        pl.semaphore_signal(barrier, inc=1, device_id={"sec": target}, device_id_type=mesh_id)
    pl.semaphore_wait(barrier, owners - 1 + sides)

    def peer_at(turn):
        return lax.rem(me + 1 + turn, owners)

    mine = pl.ds(me * local, local)
    for slot in range(slots):
        for which, source in enumerate((lesser_ref, greater_ref)):

            def send(turn, carry, slot=slot, which=which, source=source):
                peer = peer_at(turn)
                pltpu.make_async_remote_copy(
                    src_ref=source.at[:, peer, slot],
                    dst_ref=x_ref.at[slot, which, mine],
                    send_sem=in_send.at[slot],
                    recv_sem=in_recv.at[slot],
                    device_id={"el": peer},
                    device_id_type=mesh_id,
                ).start()
                return carry

            pltpu.make_async_copy(
                source.at[:, me, slot], x_ref.at[slot, which, mine], in_recv.at[slot]
            ).start()
            lax.fori_loop(0, owners - 1, send, 0)

    shared = pltpu.make_async_remote_copy(
        src_ref=coulomb_ref.at[1],
        dst_ref=other_ref,
        send_sem=c_send,
        recv_sem=c_recv,
        device_id={"sec": targets[0]},
        device_id_type=mesh_id,
    )
    shared.start()
    load_f.wait()
    load_i.wait()

    def arrive(slot):
        whole = polar_ref.at[:, :, slot]
        pltpu.make_async_copy(whole, whole, out_recv.at[slot]).wait()

    def forward_copy(slot, side):
        return pltpu.make_async_remote_copy(
            src_ref=polar_ref.at[:, :, slot],
            dst_ref=beside_refs[side].at[:, :, slot],
            send_sem=side_send.at[side, slot],
            recv_sem=side_recv.at[side, slot],
            device_id={"sec": targets[side]},
            device_id_type=mesh_id,
        )

    def pass_on(slot):
        arrive(slot)
        for side in range(sides):
            forward_copy(slot, side).start()

    for slot in range(slots):
        whole = x_ref.at[slot]
        pltpu.make_async_copy(whole, whole, in_recv.at[slot]).wait()
        d_ref[slot] = correlate_slot(
            factor, x_ref[slot, 0], x_ref[slot, 1], forward_ref, inverse_ref
        )
        pltpu.make_async_copy(
            d_ref.at[slot, mine], polar_ref.at[:, me, slot], out_recv.at[slot]
        ).start()

        def give(turn, carry, slot=slot):
            peer = peer_at(turn)
            pltpu.make_async_remote_copy(
                src_ref=d_ref.at[slot, pl.ds(peer * local, local)],
                dst_ref=polar_ref.at[:, me, slot],
                send_sem=out_send.at[slot],
                recv_sem=out_recv.at[slot],
                device_id={"el": peer},
                device_id_type=mesh_id,
            ).start()
            return carry

        lax.fori_loop(0, owners - 1, give, 0)
        if slot >= 2:
            pass_on(slot - 2)
    for slot in range(max(slots - 2, 0), slots):
        pass_on(slot)

    sent = (owners - 1) * local
    for slot in range(slots):
        part = x_ref.at[slot, :, pl.ds(0, sent)]
        pltpu.make_async_copy(part, part, in_send.at[slot]).wait()
        part = d_ref.at[slot, pl.ds(0, sent)]
        pltpu.make_async_copy(part, part, out_send.at[slot]).wait()
        for side in range(sides):
            forward_copy(slot, side).wait()
    shared.wait()


def exchange(owners, sections, lesser, greater, coulomb):
    local, count, _, width = lesser.shape
    slots = count // owners
    energies = local * owners
    sides = 1 if sections == 2 else 2
    forward, inverse = tables(energies)
    split = (local, owners, slots, 2, width)
    tile_shape = jax.ShapeDtypeStruct(split, jnp.bfloat16)
    anywhere = pl.BlockSpec(memory_space=pl.ANY)
    near = pl.BlockSpec(memory_space=pltpu.VMEM)
    dma = pltpu.SemaphoreType.DMA
    return pl.pallas_call(
        functools.partial(
            exchange_kernel, owners, sections, 1.0 / (2 * energies * energies**0.5)
        ),
        in_specs=[anywhere] * 5,
        out_specs=[near] * (2 + sides),
        out_shape=[tile_shape] * (1 + sides)
        + [jax.ShapeDtypeStruct(coulomb.shape[1:], coulomb.dtype)],
        scratch_shapes=[
            pltpu.VMEM((slots, 2, energies, 2, width), jnp.bfloat16),
            pltpu.VMEM((slots, energies, 2, width), jnp.bfloat16),
            pltpu.VMEM(forward.shape, jnp.bfloat16),
            pltpu.VMEM(inverse.shape, jnp.bfloat16),
            dma((2,)),
            dma((slots,)),
            dma((slots,)),
            dma((slots,)),
            dma((slots,)),
            dma((sides, slots)),
            dma((sides, slots)),
            dma(()),
            dma(()),
        ],
        compiler_params=pltpu.CompilerParams(
            collective_id=0, has_side_effects=True, vmem_limit_bytes=VMEM_LIMIT
        ),
    )(lesser.reshape(split), greater.reshape(split), coulomb, forward, inverse)


def screen_setup(sections, coulomb_ref, other_ref, pattern_ref, right_ref, picked_ref, mask_ref):
    terms, count, nb = mask_ref.shape
    section = lax.axis_index("sec")
    lower = other_ref[...].astype(jnp.float32).T
    upper = coulomb_ref[1].astype(jnp.float32)
    matrices = [coulomb_ref[0].astype(jnp.float32)]
    if sections == 2:
        sources = [section, 1 - section]
        matrices.append(jnp.where(section == 0, upper, lower))
    else:
        sources = [
            section,
            lax.rem(section + sections - 1, sections),
            lax.rem(section + 1, sections),
        ]
        matrices.append(jnp.where(section > 0, lower, 0.0))
        matrices.append(jnp.where(section < sections - 1, upper, 0.0))
    position = lax.broadcasted_iota(jnp.int32, (nb, TR * count), 0)
    lane = lax.broadcasted_iota(jnp.int32, (count, nb), 1) // TC
    first = lax.broadcasted_iota(jnp.int32, (count, count), 0)
    second = lax.broadcasted_iota(jnp.int32, (count, count), 1)
    across = nb // TC
    for t in range(terms):
        listed = pattern_ref[pl.ds(sources[t], 1), :]
        row = jnp.concatenate([listed // across * TR + r for r in range(TR)], axis=1)
        chosen = jnp.where(position == row, 1.0, 0.0).astype(jnp.bfloat16)
        picked_ref[t] = dot32(matrices[t].astype(jnp.bfloat16), chosen).astype(jnp.bfloat16)
        column = jnp.sum(
            jnp.where(first == second, (listed % across).astype(jnp.float32), 0.0),
            axis=1,
            keepdims=True,
        ).astype(jnp.int32)
        mask_ref[t] = jnp.where(lane == column, 1.0, 0.0).astype(jnp.bfloat16)
        right_ref[t * nb : (t + 1) * nb] = matrices[t].T.astype(jnp.bfloat16)


def screen_kernel(sections, terms, batch, *refs):
    tile_refs = refs[:terms]
    coulomb_ref, other_ref, pattern_ref, out_ref = refs[terms : terms + 4]
    right_ref, picked_ref, mask_ref, rows_ref = refs[terms + 4 :]
    _, count, nb = mask_ref.shape
    width = rows_ref.shape[-1]

    @pl.when(pl.program_id(0) == 0)
    def _():
        screen_setup(
            sections, coulomb_ref, other_ref, pattern_ref, right_ref, picked_ref, mask_ref
        )

    lane = lax.broadcasted_iota(jnp.int32, (count, width), 1) % TC
    joined = [[] for _ in range(batch * 2)]
    for t in range(terms):
        for b in range(batch):
            rows_ref[t, b] = tile_refs[t][b].reshape(2 * count, width).astype(jnp.float32)
        mask = mask_ref[t]
        for b in range(batch):
            for c in range(2):
                tile = rows_ref[t, b, pl.ds(c, count, stride=2), :]
                pieces = []
                for r in range(TR):
                    spread = jnp.take_along_axis(
                        tile, lane + r * TC, axis=1, mode="promise_in_bounds"
                    )
                    spread = spread.astype(jnp.bfloat16)
                    wide = jnp.concatenate([spread] * (nb // width), axis=1)
                    pieces.append(wide * mask)
                stacked = jnp.concatenate(pieces, axis=0)
                joined[2 * b + c].append(dot32(picked_ref[t], stacked).astype(jnp.bfloat16))
    left = jnp.concatenate([jnp.concatenate(j, axis=1) for j in joined], axis=0)
    total = dot32(left, right_ref[...]).astype(jnp.bfloat16)
    out_ref[...] = total.reshape(batch, 2, nb, nb)


def screen(sections, tiles, coulomb, other, pattern):
    terms = len(tiles)
    energies, owners, slots, _, width = tiles[0].shape
    count = owners * slots
    nb = coulomb.shape[1]
    batch = next(n for n in (8, 4, 2, 1) if energies % n == 0)
    whole = lambda array: pl.BlockSpec(array.shape, lambda i: (0,) * array.ndim)
    return pl.pallas_call(
        functools.partial(screen_kernel, sections, terms, batch),
        grid=(energies // batch,),
        in_specs=[pl.BlockSpec((batch, owners, slots, 2, width), lambda i: (i, 0, 0, 0, 0))] * terms
        + [whole(coulomb), whole(other), whole(pattern)],
        out_specs=pl.BlockSpec((batch, 2, nb, nb), lambda i: (i, 0, 0, 0)),
        out_shape=jax.ShapeDtypeStruct((energies, 2, nb, nb), jnp.bfloat16),
        scratch_shapes=[
            pltpu.VMEM((terms * nb, nb), jnp.bfloat16),
            pltpu.VMEM((terms, nb, TR * count), jnp.bfloat16),
            pltpu.VMEM((terms, count, nb), jnp.bfloat16),
            pltpu.VMEM((terms, batch, 2 * count, width), jnp.float32),
        ],
        compiler_params=pltpu.CompilerParams(vmem_limit_bytes=VMEM_LIMIT),
    )(*tiles, coulomb, other, pattern)


def on_device(sections, owners, green_lesser, green_greater, coulomb, pattern):
    _, local, count, _, width = green_lesser.shape
    polar, *beside, other = exchange(
        owners, sections, green_lesser[0], green_greater[0], coulomb[0]
    )
    screened = screen(sections, [polar, *beside], coulomb[0], other, pattern)
    return polar.reshape(1, local, count, 2, width), screened[None]


def solution(mesh):
    in_specs = (
        P("sec", "el", None, None, None),
        P("sec", "el", None, None, None),
        P("sec", None, None, None),
        P(),
    )
    out_specs = (P("sec", "el", None, None, None), P("sec", "el", None, None, None))
    return jax.shard_map(
        functools.partial(on_device, mesh.shape["sec"], mesh.shape["el"]),
        mesh=mesh,
        in_specs=in_specs,
        out_specs=out_specs,
        check_vma=False,
    )
```
